256 devices in a mesh: seq: 16 (over z, core), exp: 16 (over y, x).
Axes of the slice: x: 4, y: 4, z: 8, core: 2. Of those that a mesh axis runs over, the one named last changes fastest.
Arguments:
- tokens: bfloat16 [16, 2048, 2048], P('exp', 'seq'), may hold values from -10 to 10
- head_inputs: bfloat16 [16, 2048, 6144], P('exp', 'seq'), may hold values from -100 to 100
- window_ids: int32 [16, 2048], P('exp', 'seq'), may hold values from 0 to 3, never falling along the last dimension, each value on 1 to 1024 neighbouring positions
- modulation: float32 [16, 4, 2048], P('exp'), may hold values from -3 to 3
- out_weight: bfloat16 [2048, 2048], replicated, may hold values from -0.125 to 0.125
- expert_in: bfloat16 [16, 2048, 4096], P('exp', None, 'seq'), may hold values from -0.125 to 0.125
- expert_out: bfloat16 [16, 4096, 2048], P('exp', 'seq'), may hold values from -0.09375 to 0.09375
- expert_ids: int32 [16, 2048, 2], P('exp', 'seq'), may hold values from 0 to 15, all different within a row
- gate_probs: float32 [16, 2048, 2], P('exp', 'seq'), may hold values from 0.1 to 1
Outputs:
- block_out: bfloat16 [16, 2048, 2048], P('exp', 'seq')
The draws below stay inside these ranges and needn't reach their ends.
Inputs may be any that keep to these rules, and one draw needn't show every extreme that they name: `expert_ids`: each token names 2 different experts. `window_ids`: window numbers never fall along a clip; one window of each clip holds exactly 1024 tokens and none holds more.
All inputs are finite; a program needn't handle non-finite values.
Results may differ from the reference program's by a relative error of at most 0.014.
Values may be sent and summed in bfloat16 or wider, within the bound.
No kernel may reach another device: no remote copies, remote signals or barrier semaphores. Data moves between devices by JAX's collectives and lax.ppermute only.
A program may use at most 128 MiB of HBM per device.

```python
import math
import jax
import jax.numpy as jnp
import numpy as np
from jax import lax

D = 2048
HEADS = 32
HD = 64
FF = 4096
TOP = 2
WINDOWS = 4
TOK_DEV = 128
EXPERTS = 16
CLIPS = 16
GROUP_LEN = 2048
CAP = 12
N_SEQ = 16


def draw_tokens(key, part):
    key_values, key_rows, key_columns = jax.random.split(key, 3)
    row_scale = jnp.exp(jax.random.uniform(key_rows, (CLIPS, GROUP_LEN, 1), jnp.float32, math.log(0.2), math.log(2.0)))
    column_scale = jnp.exp(jax.random.uniform(key_columns, (1, 1, D), jnp.float32, math.log(0.2), math.log(2.0)))
    values_drawn = jnp.clip(jax.random.normal(key_values, (CLIPS, GROUP_LEN, D), jnp.float32), -2.0, 2.0)
    return (row_scale * column_scale * values_drawn).astype(jnp.bfloat16)


def draw_head_inputs(key, part):
    key_values = jax.random.fold_in(key, 0)
    drawn = jnp.clip(jax.random.normal(key_values, (CLIPS, GROUP_LEN, 3, D), jnp.float32), -6.0, 6.0)
    part_scale = jnp.array([1.5, 1.5, 1.0], jnp.float32)
    drawn = drawn * part_scale[None, None, :, None]
    return drawn.reshape(CLIPS, GROUP_LEN, 3 * D).astype(jnp.bfloat16)


def level_of(stream_key, extent, cuts, least, largest):
    level = 1.0
    for axis_at, parts in cuts:
        heights = jax.random.uniform(jax.random.fold_in(jax.random.fold_in(stream_key, 6), axis_at), (parts,), jnp.float32, least / len(cuts), largest / len(cuts))
        level = level * jnp.repeat(jnp.exp(heights), extent[axis_at] // parts).reshape((-1,) + (1,) * (len(extent) - 1 - axis_at))
    return level


def distinct(rng, rows, number_of, top, lift):
    order = jax.random.permutation(jax.random.fold_in(rng, 1), number_of)
    favour = order
    for power in range(3):
        favour = favour * favour // number_of
    favour = favour * lift // number_of
    lots = jax.random.randint(jax.random.fold_in(rng, 2), (rows, number_of), 0, 4096) + favour
    holders = jax.random.permutation(jax.random.fold_in(rng, 3), rows)[jnp.arange(number_of) % rows]
    lots = jnp.where(jnp.arange(rows)[:, None] == holders[None, :], 1 << 14, lots)
    score = lots * number_of + jnp.arange(number_of)
    return lax.top_k(score.astype(jnp.int32), top)[1].astype(jnp.int32)


def length_profile(amount, total, limit, skew):
    portions = [(1 << 20) // math.isqrt(standing ** skew) + 1 for standing in range(2, amount + 1)]
    rest, holding = total - limit - (amount - 1), [1] * (amount - 1)
    while rest > 0:
        movable = [i for i in range(amount - 1) if holding[i] < limit]
        whole, budget = sum([portions[i] for i in movable]), rest
        for i in movable:
            more = min(limit - holding[i], max(1, budget * portions[i] // whole), rest)
            holding[i] = holding[i] + more
            rest = rest - more
    return np.array([limit] + holding)


def ragged_sizes(own_key, count, total, bound, lean):
    if count == 2:
        one = jax.random.randint(own_key, (), max(1, total - bound), min(bound, total - 1) + 1)
        return jnp.stack([one, total - one])
    lengths = jnp.asarray(length_profile(count, total, bound, lean), jnp.int32)
    couples = (count - 1) // 2
    giver, receiver = lengths[1:1 + 2 * couples:2], lengths[2:2 + 2 * couples:2]
    room = jnp.minimum(giver - 1, bound - receiver)
    moved = jax.random.randint(jax.random.fold_in(own_key, 1), (couples,), 0, 1 << 20) % (room + 1)
    lengths = lengths.at[1:1 + 2 * couples:2].set(giver - moved).at[2:2 + 2 * couples:2].set(receiver + moved)
    return lengths[jax.random.permutation(jax.random.fold_in(own_key, 2), count)]


def centred(stream_key, extent, scale, most, cuts=(), kind=jnp.bfloat16):
    values = jax.random.normal(stream_key, extent, jnp.float32) * scale
    if len(cuts) > 0:
        values = level_of(stream_key, extent, cuts, -0.22, 0.18) * values
    return jnp.clip(values, min=-most, max=most).astype(kind)


def setup_inputs(seed: int = 0) -> dict:
    seeds = jax.random.split(jax.random.key(seed), 10)
    return {
        "tokens": draw_tokens(jax.random.fold_in(seeds[9], 71), 0),
        "head_inputs": draw_head_inputs(jax.random.fold_in(seeds[9], 71), 0),
        "window_ids": jax.vmap(lambda own: jnp.searchsorted(jnp.cumsum(ragged_sizes(own, WINDOWS, GROUP_LEN, GROUP_LEN // 2, 1)), jnp.arange(GROUP_LEN), side="right"))(jax.random.split(seeds[2], CLIPS)).reshape((CLIPS, GROUP_LEN)).astype(jnp.int32),
        "modulation": centred(seeds[3], (CLIPS, 4, D), 1.0, 3.0, ((0, 16),), jnp.float32),
        "out_weight": centred(seeds[4], (D, D), D ** -0.5, 0.125),
        "expert_in": centred(seeds[5], (EXPERTS, D, FF), D ** -0.5, 0.125, ((0, 16), (2, 16))),
        "expert_out": centred(seeds[6], (EXPERTS, FF, D), FF ** -0.5, 0.09375, ((0, 16), (1, 16))),
        "expert_ids": distinct(seeds[7], CLIPS * GROUP_LEN, EXPERTS, TOP, 1024).reshape((CLIPS, GROUP_LEN, TOP)),
        "gate_probs": jnp.clip(0.1 + 0.9 * jax.random.uniform(seeds[8], (CLIPS, GROUP_LEN, TOP), jnp.float32) ** level_of(seeds[8], (CLIPS, GROUP_LEN, TOP), ((0, 16), (1, 16)), -0.2, 0.2), 0.1, 1.0),
    }


def attend_clip(clip_inputs, clip_windows):
    split_heads = clip_inputs.reshape(GROUP_LEN, 3, HEADS, HD)
    per_head = jnp.transpose(split_heads, (2, 1, 0, 3))
    same_window = clip_windows[:, None] == clip_windows[None, :]
    scaling = float(HD) ** (-0.5)

    def one_head(head_block):
        scores = jnp.dot(head_block[0], head_block[1].T, preferred_element_type=jnp.float32) * scaling
        scores = jnp.where(same_window, scores, -jnp.inf)
        row_max = lax.optimization_barrier(jnp.max(scores, axis=1, keepdims=True))
        raised = jnp.exp(scores - row_max)
        weights = (raised / lax.optimization_barrier(jnp.sum(raised, axis=1, keepdims=True))).astype(jnp.bfloat16)
        return jnp.dot(weights, head_block[2], preferred_element_type=jnp.float32).astype(jnp.bfloat16)
    outputs = lax.map(one_head, per_head)
    return jnp.transpose(outputs, (1, 0, 2)).reshape(GROUP_LEN, HEADS * HD)

def reference(tokens, head_inputs, window_ids, modulation, out_weight, expert_in, expert_out, expert_ids, gate_probs):
    attended = lax.map(lambda block_pair: attend_clip(block_pair[0], block_pair[1]), (head_inputs, window_ids))
    projected = jnp.dot(attended.reshape(CLIPS * GROUP_LEN, D), out_weight, preferred_element_type=jnp.float32)
    projected = projected.reshape(CLIPS, GROUP_LEN, D)
    mixed_rows = tokens.astype(jnp.float32) + modulation[:, 0][:, None, :] * projected
    center = lax.optimization_barrier(jnp.mean(mixed_rows, axis=-1, keepdims=True))
    spread = lax.optimization_barrier(jnp.mean(jnp.square(mixed_rows - center), axis=-1, keepdims=True))
    normed = (mixed_rows - center) * lax.rsqrt(spread + 1e-06)
    normed = (normed * (1.0 + modulation[:, 2][:, None, :]) + modulation[:, 1][:, None, :]).astype(jnp.bfloat16)
    pair_experts = expert_ids.reshape(CLIPS, N_SEQ, TOK_DEV * TOP)
    onehot = (pair_experts[..., None] == jnp.arange(EXPERTS, dtype=jnp.int32)).astype(jnp.int32)
    before = jnp.cumsum(onehot, axis=2) - onehot
    slot_index = lax.optimization_barrier(jnp.sum(before * onehot, axis=3)).astype(jnp.int32)
    kept_pair = slot_index < CAP
    slot_safe = jnp.minimum(slot_index, CAP - 1).astype(jnp.int32)
    drop_slot = jnp.where(kept_pair, slot_index, CAP).astype(jnp.int32)
    clip_index = jnp.broadcast_to(jnp.arange(CLIPS, dtype=jnp.int32)[:, None, None], pair_experts.shape)
    block_index = jnp.broadcast_to(jnp.arange(N_SEQ, dtype=jnp.int32)[None, :, None], pair_experts.shape)
    token_rows = jnp.repeat(normed.reshape(CLIPS, N_SEQ, TOK_DEV, D), TOP, axis=2)
    buffers = jnp.zeros((EXPERTS, N_SEQ, CLIPS, CAP, D), jnp.bfloat16)
    buffers = buffers.at[pair_experts, block_index, clip_index, drop_slot].set(token_rows, mode='drop')
    groups = FF // N_SEQ

    def run_expert(operands):
        expert_slab, first_weight, second_weight = operands
        flat_rows = expert_slab.reshape(N_SEQ * CLIPS * CAP, D)
        hidden = jax.nn.gelu(jnp.dot(flat_rows, first_weight, preferred_element_type=jnp.float32), approximate=True).astype(jnp.bfloat16)
        pieces = jnp.einsum('rgf,gfd->grd', hidden.reshape(N_SEQ * CLIPS * CAP, N_SEQ, groups).astype(jnp.float32), second_weight.reshape(N_SEQ, groups, D).astype(jnp.float32))
        rounded = lax.optimization_barrier(pieces.astype(jnp.bfloat16)).astype(jnp.float32)
        return lax.optimization_barrier(jnp.sum(rounded, axis=0)).astype(jnp.bfloat16).reshape(N_SEQ, CLIPS, CAP, D)
    results = lax.map(run_expert, (buffers, expert_in, expert_out))
    picked = results[pair_experts, block_index, clip_index, slot_safe]
    weight = jnp.where(kept_pair, gate_probs.reshape(CLIPS, N_SEQ, TOK_DEV * TOP), 0.0)
    combined = (picked.astype(jnp.float32) * weight[..., None]).reshape(CLIPS, N_SEQ, TOK_DEV, TOP, D)
    combined = lax.optimization_barrier(jnp.sum(combined, axis=3)).reshape(CLIPS, GROUP_LEN, D)
    return (mixed_rows + modulation[:, 3][:, None, :] * combined).astype(jnp.bfloat16)
```

```python
import jax
import jax.numpy as jnp
from jax import lax
from jax.sharding import Mesh
from jax.sharding import PartitionSpec as P

HD = 64
TOP = 2
SEQ = ("z", "c")


def step_along(array, axis, shift):
    length = lax.axis_size(axis)
    return lax.ppermute(array, axis, [(i, (i + shift) % length) for i in range(length)])


def ring(first, second):
    up, down = [(first, second)], [(first, second)]
    for _ in range(3):
        up.append(tuple(step_along(w, "z", 1) for w in up[-1]))
        down.append(tuple(step_along(w, "z", -1) for w in down[-1]))
    far = (step_along(down[3][0], "z", -1), step_along(up[3][1], "z", 1))
    return [up[0], up[1], down[1], up[2], down[2], up[3], down[3], far]


def attend_block(query_block, window_block, keys_all, values_all, windows_all, scaling):
    same_window = window_block[:, None] == windows_all[None, :]
    scores = (
        jnp.einsum("qhd,khd->hqk", query_block, keys_all, preferred_element_type=jnp.float32)
        * scaling
    )
    scores = jnp.where(same_window[None], scores, -jnp.inf)
    row_max = jnp.max(scores, axis=2, keepdims=True)
    raised = jnp.exp(scores - row_max)
    weights = (raised / jnp.sum(raised, axis=2, keepdims=True)).astype(jnp.bfloat16)
    return jnp.einsum(
        "hqk,khd->qhd", weights, values_all, preferred_element_type=jnp.float32
    ).astype(jnp.bfloat16)


def attention(by_heads, windows_all):
    group_len = by_heads.shape[0]
    heads = by_heads.shape[-1] // HD
    queries = by_heads[:, 0, 0].reshape(group_len, heads, HD)
    keys_all = by_heads[:, 1, 0].reshape(group_len, heads, HD)
    values_all = by_heads[:, 2, 0].reshape(group_len, heads, HD)
    scaling = float(HD) ** (-0.5)
    parts = []
    for start in range(0, group_len, 512):
        stop = start + 512
        parts.append(
            attend_block(
                queries[start:stop],
                windows_all[start:stop],
                keys_all,
                values_all,
                windows_all,
                scaling,
            )
        )
    return jnp.concatenate(parts, axis=0).reshape(group_len, heads * HD)


def on_device(
    tokens,
    head_inputs,
    window_ids,
    modulation,
    out_weight,
    expert_in,
    expert_out,
    expert_ids,
    gate_probs,
):
    seq_count = lax.axis_size(SEQ)
    expert_count = lax.axis_size("exp")
    token_count = tokens.shape[1]
    model_width = tokens.shape[2]
    group_width = head_inputs.shape[2] // 3 // seq_count
    arranged = head_inputs[0].reshape(token_count, 3, seq_count, group_width)
    by_heads = lax.all_to_all(arranged, SEQ, split_axis=2, concat_axis=0, tiled=True)
    sent_ids = jnp.broadcast_to(window_ids[0].astype(jnp.bfloat16), (seq_count, token_count))
    windows_all = lax.all_to_all(sent_ids[:, None], SEQ, 0, 0, tiled=True).reshape(-1)
    shards = ring(expert_in[0], expert_out[0])
    attended = attention(by_heads, windows_all)
    by_tokens = lax.all_to_all(
        attended.reshape(seq_count, token_count, group_width), SEQ, 0, 0, tiled=True
    )
    by_tokens = jnp.moveaxis(by_tokens, 0, 1).reshape(token_count, model_width)
    mod_rows = modulation[0]
    projected = jnp.dot(by_tokens, out_weight, preferred_element_type=jnp.float32)
    mixed_rows = tokens[0].astype(jnp.float32) + mod_rows[0][None, :] * projected
    center = jnp.mean(mixed_rows, axis=-1, keepdims=True)
    spread = jnp.mean(jnp.square(mixed_rows - center), axis=-1, keepdims=True)
    normed = (mixed_rows - center) * lax.rsqrt(spread + 1e-06)
    normed = (normed * (1.0 + mod_rows[2][None, :]) + mod_rows[1][None, :]).astype(jnp.bfloat16)
    capacity = 3 * token_count * TOP // (4 * expert_count)
    pair_experts = expert_ids[0].reshape(token_count * TOP)
    onehot = (pair_experts[:, None] == jnp.arange(expert_count, dtype=jnp.int32)[None, :]).astype(
        jnp.int32
    )
    before = jnp.cumsum(onehot, axis=0) - onehot
    slot_index = jnp.sum(before * onehot, axis=1)
    kept_pair = slot_index < capacity
    target = pair_experts * capacity + jnp.minimum(slot_index, capacity - 1)
    slot_rows = expert_count * capacity
    matches = (target[None, :] == jnp.arange(slot_rows, dtype=jnp.int32)[:, None]) & kept_pair[
        None, :
    ]
    dispatch = jnp.sum(
        matches.reshape(slot_rows, token_count, TOP).astype(jnp.int32), axis=2
    ).astype(jnp.bfloat16)
    outgoing = jnp.dot(dispatch, normed, preferred_element_type=jnp.float32).astype(jnp.bfloat16)
    outgoing = outgoing.reshape(expert_count, capacity, model_width)
    arrived = lax.all_to_all(outgoing, "exp", split_axis=0, concat_axis=0, tiled=True).reshape(
        slot_rows, model_width
    )
    rows = jnp.concatenate([arrived, step_along(arrived, "c", 1)], axis=0)
    total = None
    for first_weight, second_weight in shards:
        hidden = jax.nn.gelu(
            jnp.dot(rows, first_weight, preferred_element_type=jnp.float32), approximate=True
        ).astype(jnp.bfloat16)
        part = jnp.dot(hidden, second_weight, preferred_element_type=jnp.float32)
        total = part if total is None else total + part
    theirs = step_along(total[slot_rows:].astype(jnp.bfloat16), "c", 1)
    summed = (total[:slot_rows] + theirs.astype(jnp.float32)).astype(jnp.bfloat16)
    outbound = summed.reshape(expert_count, capacity, model_width)
    returned = lax.all_to_all(outbound, "exp", split_axis=0, concat_axis=0, tiled=True).reshape(
        slot_rows, model_width
    )
    weight = jnp.where(kept_pair, gate_probs[0].reshape(token_count * TOP), 0.0)
    spread_weight = jnp.sum(
        jnp.where(matches, weight[None, :], 0.0).reshape(slot_rows, token_count, TOP), axis=2
    )
    coarse = spread_weight.astype(jnp.bfloat16)
    fine = (spread_weight - coarse.astype(jnp.float32)).astype(jnp.bfloat16)
    combined = jnp.einsum(
        "st,sd->td", coarse, returned, preferred_element_type=jnp.float32
    ) + jnp.einsum("st,sd->td", fine, returned, preferred_element_type=jnp.float32)
    result = (mixed_rows + mod_rows[3][None, :] * combined).astype(jnp.bfloat16)
    return result.reshape(1, token_count, model_width)


def solution(mesh):
    split = Mesh(mesh.devices.reshape(8, 2, mesh.shape["exp"]), ("z", "c", "exp"))
    in_specs = (
        P("exp", SEQ, None),
        P("exp", SEQ, None),
        P("exp", SEQ),
        P("exp", None, None),
        P(),
        P("exp", None, SEQ),
        P("exp", SEQ, None),
        P("exp", SEQ, None),
        P("exp", SEQ, None),
    )
    out_specs = P("exp", SEQ, None)
    return jax.shard_map(
        on_device, mesh=split, in_specs=in_specs, out_specs=out_specs, check_vma=False
    )
```

```python
import jax
import jax.numpy as jnp
from jax import lax
from jax.experimental import pallas as pl
from jax.experimental.pallas import tpu as pltpu
from jax.sharding import Mesh
from jax.sharding import PartitionSpec as P

HD = 64
Z = ("zh", "zl")
SEQ = ("zh", "zl", "c")
FAR = ("zh", "exp")
ROW = 8
EXTRA = 4
QB = 512
KB = 512
FLOOR = -1e30
VM = pl.BlockSpec(memory_space=pltpu.VMEM)


def step_along(array, axis, shift):
    length = lax.axis_size(axis)
    return lax.ppermute(array, axis, [(i, (i + shift) % length) for i in range(length)])


def pack_kernel(x_ref, ids_ref, o_ref):
    for i in range(o_ref.shape[0]):
        for j in range(3):
            lanes = pl.ds((16 * j + i) * 128, 128)
            o_ref[i, 128 * j : 128 * (j + 1), :] = x_ref[:, lanes]
        o_ref[i, 384:392, :] = jnp.broadcast_to(ids_ref[...].astype(jnp.float32), (8, 128)).astype(
            jnp.bfloat16
        )


def pack(head_inputs, window_ids):
    return pl.pallas_call(
        pack_kernel,
        out_shape=jax.ShapeDtypeStruct((16, 392, 128), jnp.bfloat16),
        in_specs=[VM, VM],
        out_specs=VM,
        name="pack",
    )(head_inputs, window_ids)


def attend_kernel(x_ref, o_ref, s_ref, top_ref, sum_ref, acc_ref):
    blocks, _, lanes = x_ref.shape
    tokens = blocks * 128
    ids = x_ref[:, 384:392, :][:, 0, :].astype(jnp.float32)
    edges = [jnp.sum((ids < w + 0.5).astype(jnp.float32)).astype(jnp.int32) for w in range(3)]
    first = lax.broadcasted_iota(jnp.int32, (QB, lanes), 1) < HD

    def window_of(p):
        lo, hi = edges[2], tokens
        for w in (2, 1, 0):
            inside = p < edges[w]
            lo = jnp.where(inside, edges[w - 1] if w else 0, lo)
            hi = jnp.where(inside, edges[w], hi)
        return lo, hi

    @pl.loop(0, tokens // QB)
    def _(qi):
        start = qi * QB
        q = x_ref[pl.ds(qi * (QB // 128), QB // 128), 0:128, :].reshape(QB, lanes)
        q = q * jnp.bfloat16(float(HD) ** (-0.5))
        zero = jnp.zeros_like(q)
        q2 = jnp.concatenate([jnp.where(first, q, zero), jnp.where(first, zero, q)], axis=0)
        low, _ = window_of(start)
        _, high = window_of(start + QB - 1)
        begin = low // KB
        end = (high + KB - 1) // KB
        pos = start + lax.broadcasted_iota(jnp.int32, (QB, 1), 0)
        lo, hi = window_of(jnp.concatenate([pos, pos], axis=0))
        top_ref[...] = jnp.full_like(top_ref, FLOOR)

        @pl.loop(begin, end)
        def _(kb):
            k = x_ref[pl.ds(kb * (KB // 128), KB // 128), 128:256, :].reshape(KB, lanes)
            s = lax.dot_general(
                q2, k, (((1,), (1,)), ((), ())), preferred_element_type=jnp.float32
            )
            at = kb * KB + lax.broadcasted_iota(jnp.int32, (1, KB), 1)
            s = jnp.where((at >= lo) & (at < hi), s, FLOOR)
            s_ref[kb] = s
            best = s[:, 0:128]
            for j in range(1, KB // 128):
                best = jnp.maximum(best, s[:, j * 128 : (j + 1) * 128])
            top_ref[...] = jnp.maximum(top_ref[...], best)

        top = jnp.max(top_ref[...], axis=1, keepdims=True)
        sum_ref[...] = jnp.zeros_like(sum_ref)
        acc_ref[...] = jnp.zeros_like(acc_ref)

        @pl.loop(begin, end)
        def _(kb):
            v = x_ref[pl.ds(kb * (KB // 128), KB // 128), 256:384, :].reshape(KB, lanes)
            p = jnp.exp(s_ref[kb] - top)
            part = p[:, 0:128]
            for j in range(1, KB // 128):
                part = part + p[:, j * 128 : (j + 1) * 128]
            sum_ref[...] += part
            acc_ref[...] += jnp.dot(p.astype(jnp.bfloat16), v, preferred_element_type=jnp.float32)

        out = acc_ref[...] / jnp.sum(sum_ref[...], axis=1, keepdims=True)
        out = jnp.where(first, out[:QB], out[QB:]).astype(jnp.bfloat16)
        o_ref[pl.ds(qi * (QB // 128), QB // 128)] = out.reshape(QB // 128, 128, lanes)


def attend(x):
    blocks, _, lanes = x.shape
    return pl.pallas_call(
        attend_kernel,
        out_shape=jax.ShapeDtypeStruct((blocks, 128, lanes), jnp.bfloat16),
        in_specs=[VM],
        out_specs=VM,
        scratch_shapes=[
            pltpu.VMEM((blocks * 128 // KB, 2 * QB, KB), jnp.float32),
            pltpu.VMEM((2 * QB, 128), jnp.float32),
            pltpu.VMEM((2 * QB, 128), jnp.float32),
            pltpu.VMEM((2 * QB, lanes), jnp.float32),
        ],
        compiler_params=pltpu.CompilerParams(vmem_limit_bytes=18 << 20),
        cost_estimate=pl.CostEstimate(
            flops=2 << 30, bytes_accessed=3 << 20, transcendentals=4 << 20
        ),
        name="attend",
    )(x)


def half_rows(half, width):
    row = lax.broadcasted_iota(jnp.int32, (width // 2, width), 0)
    col = lax.broadcasted_iota(jnp.int32, (width // 2, width), 1)
    same = ((col >> 3) == (row >> 2)) & ((col & 7) == (row & 3) + 4 * half)
    return same.astype(jnp.float32).astype(jnp.bfloat16)


def project_kernel(
    a_ref,
    w_ref,
    tokens_ref,
    mod_ref,
    d_ref,
    mixed_ref,
    o_ref,
    rows_ref,
    normed_ref,
    w_buf,
    sems,
):
    width = tokens_ref.shape[1]
    half = width // 2
    for n in range(width // 256):
        pltpu.make_async_copy(
            w_ref.at[:, 256 * n : 256 * (n + 1)], w_buf.at[n], sems.at[n]
        ).start()
    for i in range(a_ref.shape[0]):
        rows_ref[:, 128 * i : 128 * (i + 1)] = a_ref[i]

    @pl.loop(0, width // 256)
    def _(n):
        cols = pl.ds(pl.multiple_of(256 * n, 256), 256)
        pltpu.make_async_copy(w_buf.at[n], w_buf.at[n], sems.at[n]).wait()
        projected = jnp.dot(rows_ref[...], w_buf[n], preferred_element_type=jnp.float32)
        mixed_ref[:, cols] = (
            tokens_ref[:, cols].astype(jnp.float32) + mod_ref[0:1, cols] * projected
        )

    mixed = mixed_ref[...]
    center = jnp.mean(mixed, axis=1, keepdims=True)
    shifted = mixed - center
    spread = jnp.mean(shifted * shifted, axis=1, keepdims=True)
    normed = shifted * lax.rsqrt(spread + 1e-06)
    normed = normed * (1.0 + mod_ref[2:3, :]) + mod_ref[1:2, :]
    normed_ref[...] = normed.astype(jnp.bfloat16)
    main = d_ref.shape[0] // 2
    lower = (lax.broadcasted_iota(jnp.int32, (main, 256), 0) & EXTRA) == 0

    @pl.loop(0, half // 256)
    def _(n):
        left = pl.ds(pl.multiple_of(256 * n, 256), 256)
        right = pl.ds(pl.multiple_of(256 * n + half, 256), 256)
        last = pl.ds(pl.multiple_of(256 * n + width, 256), 256)
        first = jnp.dot(d_ref[...], normed_ref[:, left], preferred_element_type=jnp.float32)
        second = jnp.dot(d_ref[...], normed_ref[:, right], preferred_element_type=jnp.float32)
        extra = jnp.where(lower, first[main:], second[main:])
        for cols, rows in ((left, first[:main]), (right, second[:main]), (last, extra)):
            packed = rows.astype(jnp.bfloat16).reshape(main // ROW, ROW, 256)
            for copy in range(2):
                o_ref[pl.ds(copy * (main // ROW), main // ROW), :, cols] = packed


def project_and_slot(attended, out_weight, tokens, mod_rows, dispatch):
    rows, width = tokens.shape
    return pl.pallas_call(
        project_kernel,
        out_shape=(
            jax.ShapeDtypeStruct((rows, width), jnp.float32),
            jax.ShapeDtypeStruct((2 * dispatch.shape[0] // 16, ROW, 3 * width // 2), jnp.bfloat16),
        ),
        in_specs=[VM, pl.BlockSpec(memory_space=pl.ANY), VM, VM, VM],
        out_specs=(VM, VM),
        scratch_shapes=[
            pltpu.VMEM((rows, width), jnp.bfloat16),
            pltpu.VMEM((rows, width), jnp.bfloat16),
            pltpu.VMEM((width // 256, width, 256), jnp.bfloat16),
            pltpu.SemaphoreType.DMA((width // 256,)),
        ],
        compiler_params=pltpu.CompilerParams(vmem_limit_bytes=53 << 20),
        cost_estimate=pl.CostEstimate(
            flops=1 << 30, bytes_accessed=12 << 20, transcendentals=1 << 10
        ),
        name="project_and_slot",
    )(attended, out_weight, tokens, mod_rows, dispatch)


def fetch(sources, target, sems):
    return [
        pltpu.make_async_copy(source, target.at[j], sems.at[j])
        for j, source in enumerate(sources)
    ]


def activate(v):
    inner = 0.7978845608028654 * (v + 0.044715 * (v * v * v))
    return (0.5 * v * (1.0 + jnp.tanh(inner))).astype(jnp.bfloat16)


def expert_kernel(x_ref, *refs):
    count = 8
    firsts, seconds = refs[:count], refs[count : 2 * count]
    o_ref, first_buf, second_buf, rows_ref, hidden_ref, out_ref, sems = refs[2 * count :]
    blocks, _, packed = x_ref.shape
    main, width = blocks * ROW, 2048
    half = width // 2
    first_copies = fetch(firsts, first_buf, sems.at[0])
    second_copies = fetch(seconds, second_buf, sems.at[1])
    for copy in first_copies + second_copies:
        copy.start()
    rows_ref[0:main, :] = x_ref[:, :, 0:width].reshape(main, width)
    extra = x_ref[:, :, width:packed].reshape(main, half)
    for h in range(2):
        rows_ref[main:, h * half : (h + 1) * half] = jnp.dot(
            half_rows(h, main), extra, preferred_element_type=jnp.float32
        ).astype(jnp.bfloat16)

    @pl.loop(0, count)
    def _(j):
        pltpu.make_async_copy(first_buf.at[j], first_buf.at[j], sems.at[0, j]).wait()
        v = jnp.dot(rows_ref[...], first_buf[j], preferred_element_type=jnp.float32)
        hidden_ref[:, pl.ds(pl.multiple_of(256 * j, 256), 256)] = activate(v)

    for copy in second_copies:
        copy.wait()

    @pl.loop(0, width // 256)
    def _(n):
        cols = pl.ds(pl.multiple_of(256 * n, 256), 256)
        out_ref[:, cols] = jnp.dot(
            hidden_ref[...],
            second_buf[:, :, cols].reshape(256 * count, 256),
            preferred_element_type=jnp.float32,
        ).astype(jnp.bfloat16)

    o_ref[:, :, 0:width] = out_ref[0:main, :].reshape(blocks, ROW, width)
    back = None
    for h in range(2):
        part = lax.dot_general(
            half_rows(h, main),
            out_ref[main:, h * half : (h + 1) * half],
            (((0,), (0,)), ((), ())),
            preferred_element_type=jnp.float32,
        )
        back = part if back is None else back + part
    o_ref[:, :, width:packed] = back.astype(jnp.bfloat16).reshape(blocks, ROW, half)


def run_expert(arrived, firsts, seconds):
    rows, count = arrived.shape[0] * (ROW + EXTRA), len(firsts)
    anywhere = pl.BlockSpec(memory_space=pl.ANY)
    return pl.pallas_call(
        expert_kernel,
        out_shape=jax.ShapeDtypeStruct(arrived.shape, jnp.bfloat16),
        in_specs=[VM] + [anywhere] * (2 * count),
        out_specs=VM,
        scratch_shapes=[
            pltpu.VMEM((count, 2048, 256), jnp.bfloat16),
            pltpu.VMEM((count, 256, 2048), jnp.bfloat16),
            pltpu.VMEM((rows, 2048), jnp.bfloat16),
            pltpu.VMEM((rows, 256 * count), jnp.bfloat16),
            pltpu.VMEM((rows, 2048), jnp.bfloat16),
            pltpu.SemaphoreType.DMA((2, count)),
        ],
        compiler_params=pltpu.CompilerParams(vmem_limit_bytes=58 << 20),
        cost_estimate=pl.CostEstimate(
            flops=6 << 30, bytes_accessed=20 << 20, transcendentals=1 << 20
        ),
        name="run_expert",
    )(arrived, *firsts, *seconds)


def finish_kernel(r_ref, g_ref, mixed_ref, gate_ref, o_ref):
    width = mixed_ref.shape[1]
    half = width // 2
    gains = g_ref[...]
    coarse = gains.astype(jnp.bfloat16)
    fine = (gains - coarse.astype(jnp.float32)).astype(jnp.bfloat16)
    both = jnp.concatenate([coarse, fine], axis=0)
    tokens = mixed_ref.shape[0]
    lane = lax.broadcasted_iota(jnp.int32, (2 * tokens, 128), 1)
    zero = jnp.zeros((2 * tokens, 128), jnp.bfloat16)
    for h in range(2):
        total = None
        for zh in range(2):
            part = r_ref[16 * zh : 16 * (zh + 1)]
            main = part[:, :, h * half : (h + 1) * half].reshape(128, half)
            extra = part[:, :, width : width + half].reshape(128, half)
            chosen = jnp.where(((lane >> 2) & 1) == h, both[:, 128:], zero)
            more = jnp.dot(both[:, :128], main, preferred_element_type=jnp.float32)
            more = more + jnp.dot(chosen, extra, preferred_element_type=jnp.float32)
            total = more if total is None else total + more
        cols = slice(h * half, (h + 1) * half)
        combined = total[:tokens] + total[tokens:]
        o_ref[:, cols] = (mixed_ref[:, cols] + gate_ref[:, cols] * combined).astype(jnp.bfloat16)


def finish(returned, gains, mixed, gate):
    return pl.pallas_call(
        finish_kernel,
        out_shape=jax.ShapeDtypeStruct(mixed.shape, jnp.bfloat16),
        in_specs=[VM] * 4,
        out_specs=VM,
        compiler_params=pltpu.CompilerParams(vmem_limit_bytes=20 << 20),
        name="finish",
    )(returned, gains, mixed, gate)


def hop(array, turn):
    layers, cores = lax.axis_size(Z), lax.axis_size("c")
    pairs = []
    for z in range(layers):
        for c in range(cores):
            to = (z + (turn if c else -turn)) % layers
            pairs.append((z * cores + c, to * cores + c))
    return lax.ppermute(array, SEQ, pairs)


def gather_weights(first, second):
    pair = {"first": first, "second": second}
    ahead, behind, far = {}, {}, {}
    for name, w in pair.items():
        ahead[name] = hop(w, 1)
        behind[name] = hop(w, -1)
    for name, w in ahead.items():
        far[name] = hop(w, 1)
    gathered = []
    for name, w in pair.items():
        mine = [w, ahead[name], behind[name], far[name]]
        gathered.append(mine + [step_along(piece, "c", 1) for piece in mine])
    return gathered


def block(
    tokens,
    head_inputs,
    window_ids,
    modulation,
    out_weight,
    expert_in,
    expert_out,
    expert_ids,
    gate_probs,
):
    expert_count = lax.axis_size("exp")
    by_heads = lax.all_to_all(pack(head_inputs[0], window_ids), SEQ, 0, 0, tiled=True)
    firsts, seconds = gather_weights(expert_in[0], expert_out[0])
    attended = attend(by_heads)
    by_tokens = lax.all_to_all(attended, SEQ, 0, 0, tiled=True)
    mod_rows = modulation[0]
    pairs = expert_ids[0]
    pair_experts = pairs.reshape(-1)
    onehot = (pair_experts[:, None] == jnp.arange(expert_count, dtype=jnp.int32)[None, :]).astype(
        jnp.int32
    )
    before = jnp.cumsum(onehot, axis=0) - onehot
    slots = jnp.sum(before * onehot, axis=1).reshape(pairs.shape)
    place = jnp.arange(2 * expert_count * ROW, dtype=jnp.int32)
    owner = (place >> 3) & (expert_count - 1)
    slot = jnp.where(place < expert_count * ROW, place & 7, ROW + (place & 3))
    chosen = (pairs[None] == owner[:, None, None]) & (slots[None] == slot[:, None, None])
    dispatch = jnp.sum(chosen.astype(jnp.int32), axis=2).astype(jnp.bfloat16)
    picked = (pairs[:, :, None] == owner[None, None]) & (slots[:, :, None] == slot[None, None])
    gains = jnp.sum(jnp.where(picked, gate_probs[0][:, :, None], 0.0), axis=1)
    mixed_rows, outgoing = project_and_slot(by_tokens, out_weight, tokens[0], mod_rows, dispatch)
    arrived = lax.all_to_all(outgoing, FAR, 0, 0, tiled=True)
    outbound = run_expert(arrived, firsts, seconds)
    returned = lax.all_to_all(outbound, FAR, 0, 0, tiled=True)
    return finish(returned, gains, mixed_rows, mod_rows[3][None, :])[None]


def solution(mesh):
    split = Mesh(
        mesh.devices.reshape(2, 4, 2, mesh.shape["exp"]), ("zh", "zl", "c", "exp")
    )
    in_specs = (
        P("exp", SEQ, None),
        P("exp", SEQ, None),
        P("exp", SEQ),
        P("exp", None, None),
        P(),
        P("exp", None, SEQ),
        P("exp", SEQ, None),
        P("exp", SEQ, None),
        P("exp", SEQ, None),
    )
    out_specs = P("exp", SEQ, None)
    return jax.shard_map(block, mesh=split, in_specs=in_specs, out_specs=out_specs, check_vma=False)
```

```python
import jax
import jax.numpy as jnp
from jax import lax
from jax.experimental import pallas as pl
from jax.experimental.pallas import tpu as pltpu
from jax.sharding import Mesh
from jax.sharding import PartitionSpec as P

HD = 64
Z = ("zh", "zl")
SEQ = ("zh", "zl", "c")
FAR = ("zh", "exp")
ROW = 8
EXTRA = 4
QB = 512
KB = 512
FLOOR = -1e30
VM = pl.BlockSpec(memory_space=pltpu.VMEM)


def step_along(array, axis, shift):
    length = lax.axis_size(axis)
    return lax.ppermute(array, axis, [(i, (i + shift) % length) for i in range(length)])


def pack_kernel(x_ref, ids_ref, o_ref):
    for i in range(o_ref.shape[0]):
        for j in range(3):
            lanes = pl.ds((16 * j + i) * 128, 128)
            o_ref[i, 128 * j : 128 * (j + 1), :] = x_ref[:, lanes]
        o_ref[i, 384:392, :] = jnp.broadcast_to(ids_ref[...].astype(jnp.float32), (8, 128)).astype(
            jnp.bfloat16
        )


def pack(head_inputs, window_ids):
    return pl.pallas_call(
        pack_kernel,
        out_shape=jax.ShapeDtypeStruct((16, 392, 128), jnp.bfloat16),
        in_specs=[VM, VM],
        out_specs=VM,
        name="pack",
    )(head_inputs, window_ids)


def attend_kernel(x_ref, o_ref, s_ref, top_ref, sum_ref, acc_ref):
    blocks, _, lanes = x_ref.shape
    tokens = blocks * 128
    ids = x_ref[:, 384:392, :][:, 0, :].astype(jnp.float32)
    edges = [jnp.sum((ids < w + 0.5).astype(jnp.float32)).astype(jnp.int32) for w in range(3)]
    first = lax.broadcasted_iota(jnp.int32, (QB, lanes), 1) < HD

    def window_of(p):
        lo, hi = edges[2], tokens
        for w in (2, 1, 0):
            inside = p < edges[w]
            lo = jnp.where(inside, edges[w - 1] if w else 0, lo)
            hi = jnp.where(inside, edges[w], hi)
        return lo, hi

    @pl.loop(0, tokens // QB)
    def _(qi):
        start = qi * QB
        q = x_ref[pl.ds(qi * (QB // 128), QB // 128), 0:128, :].reshape(QB, lanes)
        q = q * jnp.bfloat16(float(HD) ** (-0.5))
        zero = jnp.zeros_like(q)
        q2 = jnp.concatenate([jnp.where(first, q, zero), jnp.where(first, zero, q)], axis=0)
        low, _ = window_of(start)
        _, high = window_of(start + QB - 1)
        begin = low // KB
        end = (high + KB - 1) // KB
        pos = start + lax.broadcasted_iota(jnp.int32, (QB, 1), 0)
        lo, hi = window_of(jnp.concatenate([pos, pos], axis=0))
        top_ref[...] = jnp.full_like(top_ref, FLOOR)

        @pl.loop(begin, end)
        def _(kb):
            k = x_ref[pl.ds(kb * (KB // 128), KB // 128), 128:256, :].reshape(KB, lanes)
            s = lax.dot_general(
                q2, k, (((1,), (1,)), ((), ())), preferred_element_type=jnp.float32
            )
            at = kb * KB + lax.broadcasted_iota(jnp.int32, (1, KB), 1)
            s = jnp.where((at >= lo) & (at < hi), s, FLOOR)
            s_ref[kb] = s
            best = s[:, 0:128]
            for j in range(1, KB // 128):
                best = jnp.maximum(best, s[:, j * 128 : (j + 1) * 128])
            top_ref[...] = jnp.maximum(top_ref[...], best)

        top = jnp.max(top_ref[...], axis=1, keepdims=True)
        sum_ref[...] = jnp.zeros_like(sum_ref)
        acc_ref[...] = jnp.zeros_like(acc_ref)

        @pl.loop(begin, end)
        def _(kb):
            v = x_ref[pl.ds(kb * (KB // 128), KB // 128), 256:384, :].reshape(KB, lanes)
            p = jnp.exp(s_ref[kb] - top)
            part = p[:, 0:128]
            for j in range(1, KB // 128):
                part = part + p[:, j * 128 : (j + 1) * 128]
            sum_ref[...] += part
            acc_ref[...] += jnp.dot(p.astype(jnp.bfloat16), v, preferred_element_type=jnp.float32)

        out = acc_ref[...] / jnp.sum(sum_ref[...], axis=1, keepdims=True)
        out = jnp.where(first, out[:QB], out[QB:]).astype(jnp.bfloat16)
        o_ref[pl.ds(qi * (QB // 128), QB // 128)] = out.reshape(QB // 128, 128, lanes)


def attend(x):
    blocks, _, lanes = x.shape
    return pl.pallas_call(
        attend_kernel,
        out_shape=jax.ShapeDtypeStruct((blocks, 128, lanes), jnp.bfloat16),
        in_specs=[VM],
        out_specs=VM,
        scratch_shapes=[
            pltpu.VMEM((blocks * 128 // KB, 2 * QB, KB), jnp.float32),
            pltpu.VMEM((2 * QB, 128), jnp.float32),
            pltpu.VMEM((2 * QB, 128), jnp.float32),
            pltpu.VMEM((2 * QB, lanes), jnp.float32),
        ],
        compiler_params=pltpu.CompilerParams(vmem_limit_bytes=18 << 20),
        cost_estimate=pl.CostEstimate(
            flops=2 << 30, bytes_accessed=3 << 20, transcendentals=4 << 20
        ),
        name="attend",
    )(x)


def half_rows(half, width):
    row = lax.broadcasted_iota(jnp.int32, (width // 2, width), 0)
    col = lax.broadcasted_iota(jnp.int32, (width // 2, width), 1)
    same = ((col >> 3) == (row >> 2)) & ((col & 7) == (row & 3) + 4 * half)
    return same.astype(jnp.float32).astype(jnp.bfloat16)


def project_kernel(
    a_ref,
    w_ref,
    tokens_ref,
    mod_ref,
    d_ref,
    mixed_ref,
    o_ref,
    rows_ref,
    normed_ref,
    w_buf,
    sems,
):
    width = tokens_ref.shape[1]
    half = width // 2
    for n in range(width // 256):
        pltpu.make_async_copy(
            w_ref.at[:, 256 * n : 256 * (n + 1)], w_buf.at[n], sems.at[n]
        ).start()
    for i in range(a_ref.shape[0]):
        rows_ref[:, 128 * i : 128 * (i + 1)] = a_ref[i]

    @pl.loop(0, width // 256)
    def _(n):
        cols = pl.ds(pl.multiple_of(256 * n, 256), 256)
        pltpu.make_async_copy(w_buf.at[n], w_buf.at[n], sems.at[n]).wait()
        projected = jnp.dot(rows_ref[...], w_buf[n], preferred_element_type=jnp.float32)
        mixed_ref[:, cols] = (
            tokens_ref[:, cols].astype(jnp.float32) + mod_ref[0:1, cols] * projected
        )

    mixed = mixed_ref[...]
    center = jnp.mean(mixed, axis=1, keepdims=True)
    shifted = mixed - center
    spread = jnp.mean(shifted * shifted, axis=1, keepdims=True)
    normed = shifted * lax.rsqrt(spread + 1e-06)
    normed = normed * (1.0 + mod_ref[2:3, :]) + mod_ref[1:2, :]
    normed_ref[...] = normed.astype(jnp.bfloat16)
    main = d_ref.shape[0] // 2
    lower = (lax.broadcasted_iota(jnp.int32, (main, 256), 0) & EXTRA) == 0

    @pl.loop(0, half // 256)
    def _(n):
        left = pl.ds(pl.multiple_of(256 * n, 256), 256)
        right = pl.ds(pl.multiple_of(256 * n + half, 256), 256)
        last = pl.ds(pl.multiple_of(256 * n + width, 256), 256)
        first = jnp.dot(d_ref[...], normed_ref[:, left], preferred_element_type=jnp.float32)
        second = jnp.dot(d_ref[...], normed_ref[:, right], preferred_element_type=jnp.float32)
        extra = jnp.where(lower, first[main:], second[main:])
        for cols, rows in ((left, first[:main]), (right, second[:main]), (last, extra)):
            packed = rows.astype(jnp.bfloat16).reshape(main // ROW, ROW, 256)
            for copy in range(2):
                o_ref[pl.ds(copy * (main // ROW), main // ROW), :, cols] = packed


def project_and_slot(attended, out_weight, tokens, mod_rows, dispatch):
    rows, width = tokens.shape
    return pl.pallas_call(
        project_kernel,
        out_shape=(
            jax.ShapeDtypeStruct((rows, width), jnp.float32),
            jax.ShapeDtypeStruct((2 * dispatch.shape[0] // 16, ROW, 3 * width // 2), jnp.bfloat16),
        ),
        in_specs=[VM, pl.BlockSpec(memory_space=pl.ANY), VM, VM, VM],
        out_specs=(VM, VM),
        scratch_shapes=[
            pltpu.VMEM((rows, width), jnp.bfloat16),
            pltpu.VMEM((rows, width), jnp.bfloat16),
            pltpu.VMEM((width // 256, width, 256), jnp.bfloat16),
            pltpu.SemaphoreType.DMA((width // 256,)),
        ],
        compiler_params=pltpu.CompilerParams(vmem_limit_bytes=53 << 20),
        cost_estimate=pl.CostEstimate(
            flops=1 << 30, bytes_accessed=12 << 20, transcendentals=1 << 10
        ),
        name="project_and_slot",
    )(attended, out_weight, tokens, mod_rows, dispatch)


def fetch(sources, target, sems):
    return [
        pltpu.make_async_copy(source, target.at[j], sems.at[j])
        for j, source in enumerate(sources)
    ]


def activate(v):
    inner = 0.7978845608028654 * (v + 0.044715 * (v * v * v))
    return (0.5 * v * (1.0 + jnp.tanh(inner))).astype(jnp.bfloat16)


def expert_kernel(x_ref, *refs):
    count = 8
    firsts, seconds = refs[:count], refs[count : 2 * count]
    o_ref, first_buf, second_buf, rows_ref, hidden_ref, out_ref, sems = refs[2 * count :]
    blocks, _, packed = x_ref.shape
    main, width = blocks * ROW, 2048
    half = width // 2
    first_copies = fetch(firsts, first_buf, sems.at[0])
    second_copies = fetch(seconds, second_buf, sems.at[1])
    for copy in first_copies + second_copies:
        copy.start()
    rows_ref[0:main, :] = x_ref[:, :, 0:width].reshape(main, width)
    extra = x_ref[:, :, width:packed].reshape(main, half)
    for h in range(2):
        rows_ref[main:, h * half : (h + 1) * half] = jnp.dot(
            half_rows(h, main), extra, preferred_element_type=jnp.float32
        ).astype(jnp.bfloat16)

    @pl.loop(0, count // 2)
    def _(i):
        for j in (2 * i, 2 * i + 1):
            pltpu.make_async_copy(first_buf.at[j], first_buf.at[j], sems.at[0, j]).wait()
        for j in (2 * i, 2 * i + 1):
            v = jnp.dot(rows_ref[...], first_buf[j], preferred_element_type=jnp.float32)
            hidden_ref[:, pl.ds(pl.multiple_of(256 * j, 256), 256)] = activate(v)

    for copy in second_copies:
        copy.wait()

    @pl.loop(0, width // 512)
    def _(i):
        for n in (2 * i, 2 * i + 1):
            cols = pl.ds(pl.multiple_of(256 * n, 256), 256)
            out_ref[:, cols] = jnp.dot(
                hidden_ref[...],
                second_buf[:, :, cols].reshape(256 * count, 256),
                preferred_element_type=jnp.float32,
            ).astype(jnp.bfloat16)

    o_ref[:, :, 0:width] = out_ref[0:main, :].reshape(blocks, ROW, width)
    back = None
    for h in range(2):
        part = lax.dot_general(
            half_rows(h, main),
            out_ref[main:, h * half : (h + 1) * half],
            (((0,), (0,)), ((), ())),
            preferred_element_type=jnp.float32,
        )
        back = part if back is None else back + part
    o_ref[:, :, width:packed] = back.astype(jnp.bfloat16).reshape(blocks, ROW, half)


def run_expert(arrived, firsts, seconds):
    rows, count = arrived.shape[0] * (ROW + EXTRA), len(firsts)
    anywhere = pl.BlockSpec(memory_space=pl.ANY)
    return pl.pallas_call(
        expert_kernel,
        out_shape=jax.ShapeDtypeStruct(arrived.shape, jnp.bfloat16),
        in_specs=[VM] + [anywhere] * (2 * count),
        out_specs=VM,
        scratch_shapes=[
            pltpu.VMEM((count, 2048, 256), jnp.bfloat16),
            pltpu.VMEM((count, 256, 2048), jnp.bfloat16),
            pltpu.VMEM((rows, 2048), jnp.bfloat16),
            pltpu.VMEM((rows, 256 * count), jnp.bfloat16),
            pltpu.VMEM((rows, 2048), jnp.bfloat16),
            pltpu.SemaphoreType.DMA((2, count)),
        ],
        compiler_params=pltpu.CompilerParams(vmem_limit_bytes=48 << 20),
        cost_estimate=pl.CostEstimate(
            flops=6 << 30, bytes_accessed=20 << 20, transcendentals=1 << 20
        ),
        name="run_expert",
    )(arrived, *firsts, *seconds)


def finish_kernel(r_ref, g_ref, mixed_ref, gate_ref, o_ref):
    width = mixed_ref.shape[1]
    half = width // 2
    gains = g_ref[...]
    coarse = gains.astype(jnp.bfloat16)
    fine = (gains - coarse.astype(jnp.float32)).astype(jnp.bfloat16)
    both = jnp.concatenate([coarse, fine], axis=0)
    tokens = mixed_ref.shape[0]
    tall = r_ref.shape[0] * ROW
    lane = lax.broadcasted_iota(jnp.int32, (2 * tokens, tall), 1)
    zero = jnp.zeros((2 * tokens, tall), jnp.bfloat16)
    extra = r_ref[:, :, width : width + half].reshape(tall, half)
    for h in range(2):
        main = r_ref[:, :, h * half : (h + 1) * half].reshape(tall, half)
        chosen = jnp.where(((lane >> 2) & 1) == h, both[:, tall:], zero)
        total = jnp.dot(both[:, :tall], main, preferred_element_type=jnp.float32)
        total = total + jnp.dot(chosen, extra, preferred_element_type=jnp.float32)
        cols = slice(h * half, (h + 1) * half)
        combined = total[:tokens] + total[tokens:]
        o_ref[:, cols] = (mixed_ref[:, cols] + gate_ref[:, cols] * combined).astype(jnp.bfloat16)


def finish(returned, gains, mixed, gate):
    return pl.pallas_call(
        finish_kernel,
        out_shape=jax.ShapeDtypeStruct(mixed.shape, jnp.bfloat16),
        in_specs=[VM] * 4,
        out_specs=VM,
        compiler_params=pltpu.CompilerParams(vmem_limit_bytes=20 << 20),
        name="finish",
    )(returned, gains, mixed, gate)


def hop(array, turn):
    layers, cores = lax.axis_size(Z), lax.axis_size("c")
    pairs = []
    for z in range(layers):
        for c in range(cores):
            to = (z + (turn if c else -turn)) % layers
            pairs.append((z * cores + c, to * cores + c))
    return lax.ppermute(array, SEQ, pairs)


def gather_weights(first, second):
    pair = {"first": first, "second": second}
    ahead, behind, far = {}, {}, {}
    for name, w in pair.items():
        ahead[name] = hop(w, 1)
        behind[name] = hop(w, -1)
    for name, w in ahead.items():
        far[name] = hop(w, 1)
    gathered = []
    for name, w in pair.items():
        mine = [w, ahead[name], behind[name], far[name]]
        gathered.append(mine + [step_along(piece, "c", 1) for piece in mine])
    return gathered


def block(
    tokens,
    head_inputs,
    window_ids,
    modulation,
    out_weight,
    expert_in,
    expert_out,
    expert_ids,
    gate_probs,
):
    expert_count = lax.axis_size("exp")
    by_heads = lax.all_to_all(pack(head_inputs[0], window_ids), SEQ, 0, 0, tiled=True)
    firsts, seconds = gather_weights(expert_in[0], expert_out[0])
    attended = attend(by_heads)
    by_tokens = lax.all_to_all(attended, SEQ, 0, 0, tiled=True)
    mod_rows = modulation[0]
    pairs = expert_ids[0]
    pair_experts = pairs.reshape(-1)
    onehot = (pair_experts[:, None] == jnp.arange(expert_count, dtype=jnp.int32)[None, :]).astype(
        jnp.int32
    )
    before = jnp.cumsum(onehot, axis=0) - onehot
    slots = jnp.sum(before * onehot, axis=1).reshape(pairs.shape)
    place = jnp.arange(2 * expert_count * ROW, dtype=jnp.int32)
    owner = (place >> 3) & (expert_count - 1)
    slot = jnp.where(place < expert_count * ROW, place & 7, ROW + (place & 3))
    chosen = (pairs[None] == owner[:, None, None]) & (slots[None] == slot[:, None, None])
    dispatch = jnp.sum(chosen.astype(jnp.int32), axis=2).astype(jnp.bfloat16)
    place = jnp.arange(4 * expert_count * ROW, dtype=jnp.int32)
    owner = (place >> 3) & (expert_count - 1)
    slot = jnp.where(place < 2 * expert_count * ROW, place & 7, ROW + (place & 3))
    picked = (pairs[:, :, None] == owner[None, None]) & (slots[:, :, None] == slot[None, None])
    gains = jnp.sum(jnp.where(picked, gate_probs[0][:, :, None], 0.0), axis=1)
    mixed_rows, outgoing = project_and_slot(by_tokens, out_weight, tokens[0], mod_rows, dispatch)
    arrived = lax.all_to_all(outgoing, FAR, 0, 0, tiled=True)
    outbound = run_expert(arrived, firsts, seconds)
    returned = lax.all_to_all(outbound, FAR, 0, 0, tiled=True)
    return finish(returned, gains, mixed_rows, mod_rows[3][None, :])[None]


def solution(mesh):
    split = Mesh(
        mesh.devices.reshape(2, 4, 2, mesh.shape["exp"]), ("zh", "zl", "c", "exp")
    )
    in_specs = (
        P("exp", SEQ, None),
        P("exp", SEQ, None),
        P("exp", SEQ),
        P("exp", None, None),
        P(),
        P("exp", None, SEQ),
        P("exp", SEQ, None),
        P("exp", SEQ, None),
        P("exp", SEQ, None),
    )
    out_specs = P("exp", SEQ, None)
    return jax.shard_map(block, mesh=split, in_specs=in_specs, out_specs=out_specs, check_vma=False)
```

```python
import jax
import jax.numpy as jnp
from jax import lax
from jax.experimental import pallas as pl
from jax.experimental.pallas import tpu as pltpu
from jax.sharding import Mesh
from jax.sharding import PartitionSpec as P

HD = 64
Z = ("zh", "zl")
SEQ = ("zh", "zl", "c")
FAR = ("zh", "exp")
ROW = 8
EXTRA = 4
QB = 512
KB = 512
FLOOR = -1e30
VM = pl.BlockSpec(memory_space=pltpu.VMEM)


def step_along(array, axis, shift):
    length = lax.axis_size(axis)
    return lax.ppermute(array, axis, [(i, (i + shift) % length) for i in range(length)])


def pack_kernel(x_ref, ids_ref, o_ref):
    for i in range(o_ref.shape[0]):
        for j in range(3):
            lanes = pl.ds((16 * j + i) * 128, 128)
            o_ref[i, 128 * j : 128 * (j + 1), :] = x_ref[:, lanes]
        o_ref[i, 384:392, :] = jnp.broadcast_to(ids_ref[...].astype(jnp.float32), (8, 128)).astype(
            jnp.bfloat16
        )


def pack(head_inputs, window_ids):
    return pl.pallas_call(
        pack_kernel,
        out_shape=jax.ShapeDtypeStruct((16, 392, 128), jnp.bfloat16),
        in_specs=[VM, VM],
        out_specs=VM,
        name="pack",
    )(head_inputs, window_ids)


def attend_kernel(x_ref, o_ref, s_ref, top_ref, sum_ref, acc_ref):
    blocks, _, lanes = x_ref.shape
    tokens = blocks * 128
    ids = x_ref[:, 384:392, :][:, 0, :].astype(jnp.float32)
    edges = [jnp.sum((ids < w + 0.5).astype(jnp.float32)).astype(jnp.int32) for w in range(3)]
    first = lax.broadcasted_iota(jnp.int32, (QB, lanes), 1) < HD

    def window_of(p):
        lo, hi = edges[2], tokens
        for w in (2, 1, 0):
            inside = p < edges[w]
            lo = jnp.where(inside, edges[w - 1] if w else 0, lo)
            hi = jnp.where(inside, edges[w], hi)
        return lo, hi

    @pl.loop(0, tokens // QB)
    def _(qi):
        start = qi * QB
        q = x_ref[pl.ds(qi * (QB // 128), QB // 128), 0:128, :].reshape(QB, lanes)
        q = q * jnp.bfloat16(float(HD) ** (-0.5))
        zero = jnp.zeros_like(q)
        q2 = jnp.concatenate([jnp.where(first, q, zero), jnp.where(first, zero, q)], axis=0)
        low, _ = window_of(start)
        _, high = window_of(start + QB - 1)
        begin = low // KB
        end = (high + KB - 1) // KB
        pos = start + lax.broadcasted_iota(jnp.int32, (QB, 1), 0)
        lo, hi = window_of(jnp.concatenate([pos, pos], axis=0))
        top_ref[...] = jnp.full_like(top_ref, FLOOR)

        @pl.loop(begin, end)
        def _(kb):
            k = x_ref[pl.ds(kb * (KB // 128), KB // 128), 128:256, :].reshape(KB, lanes)
            s = lax.dot_general(
                q2, k, (((1,), (1,)), ((), ())), preferred_element_type=jnp.float32
            )
            at = kb * KB + lax.broadcasted_iota(jnp.int32, (1, KB), 1)
            s = jnp.where((at >= lo) & (at < hi), s, FLOOR)
            s_ref[kb] = s
            best = s[:, 0:128]
            for j in range(1, KB // 128):
                best = jnp.maximum(best, s[:, j * 128 : (j + 1) * 128])
            top_ref[...] = jnp.maximum(top_ref[...], best)

        top = jnp.max(top_ref[...], axis=1, keepdims=True)
        sum_ref[...] = jnp.zeros_like(sum_ref)
        acc_ref[...] = jnp.zeros_like(acc_ref)

        @pl.loop(begin, end)
        def _(kb):
            v = x_ref[pl.ds(kb * (KB // 128), KB // 128), 256:384, :].reshape(KB, lanes)
            p = jnp.exp(s_ref[kb] - top)
            part = p[:, 0:128]
            for j in range(1, KB // 128):
                part = part + p[:, j * 128 : (j + 1) * 128]
            sum_ref[...] += part
            acc_ref[...] += jnp.dot(p.astype(jnp.bfloat16), v, preferred_element_type=jnp.float32)

        out = acc_ref[...] / jnp.sum(sum_ref[...], axis=1, keepdims=True)
        out = jnp.where(first, out[:QB], out[QB:]).astype(jnp.bfloat16)
        o_ref[pl.ds(qi * (QB // 128), QB // 128)] = out.reshape(QB // 128, 128, lanes)


def attend(x):
    blocks, _, lanes = x.shape
    return pl.pallas_call(
        attend_kernel,
        out_shape=jax.ShapeDtypeStruct((blocks, 128, lanes), jnp.bfloat16),
        in_specs=[VM],
        out_specs=VM,
        scratch_shapes=[
            pltpu.VMEM((blocks * 128 // KB, 2 * QB, KB), jnp.float32),
            pltpu.VMEM((2 * QB, 128), jnp.float32),
            pltpu.VMEM((2 * QB, 128), jnp.float32),
            pltpu.VMEM((2 * QB, lanes), jnp.float32),
        ],
        compiler_params=pltpu.CompilerParams(vmem_limit_bytes=18 << 20),
        cost_estimate=pl.CostEstimate(
            flops=2 << 30, bytes_accessed=3 << 20, transcendentals=4 << 20
        ),
        name="attend",
    )(x)


def half_rows(half, width):
    row = lax.broadcasted_iota(jnp.int32, (width // 2, width), 0)
    col = lax.broadcasted_iota(jnp.int32, (width // 2, width), 1)
    same = ((col >> 3) == (row >> 2)) & ((col & 7) == (row & 3) + 4 * half)
    return same.astype(jnp.float32).astype(jnp.bfloat16)


def project_kernel(
    a_ref,
    w_ref,
    tokens_ref,
    mod_ref,
    d_ref,
    mixed_ref,
    o_ref,
    rows_ref,
    normed_ref,
    w_buf,
    sems,
):
    width = tokens_ref.shape[1]
    half = width // 2
    for n in range(width // 256):
        pltpu.make_async_copy(
            w_ref.at[:, 256 * n : 256 * (n + 1)], w_buf.at[n], sems.at[n]
        ).start()
    for i in range(a_ref.shape[0]):
        rows_ref[:, 128 * i : 128 * (i + 1)] = a_ref[i]

    @pl.loop(0, width // 256)
    def _(n):
        cols = pl.ds(pl.multiple_of(256 * n, 256), 256)
        pltpu.make_async_copy(w_buf.at[n], w_buf.at[n], sems.at[n]).wait()
        projected = jnp.dot(rows_ref[...], w_buf[n], preferred_element_type=jnp.float32)
        mixed_ref[:, cols] = (
            tokens_ref[:, cols].astype(jnp.float32) + mod_ref[0:1, cols] * projected
        )

    mixed = mixed_ref[...]
    center = jnp.mean(mixed, axis=1, keepdims=True)
    shifted = mixed - center
    spread = jnp.mean(shifted * shifted, axis=1, keepdims=True)
    normed = shifted * lax.rsqrt(spread + 1e-06)
    normed = normed * (1.0 + mod_ref[2:3, :]) + mod_ref[1:2, :]
    normed_ref[...] = normed.astype(jnp.bfloat16)
    main = d_ref.shape[0] // 2
    lower = (lax.broadcasted_iota(jnp.int32, (main, 256), 0) & EXTRA) == 0

    @pl.loop(0, half // 256)
    def _(n):
        left = pl.ds(pl.multiple_of(256 * n, 256), 256)
        right = pl.ds(pl.multiple_of(256 * n + half, 256), 256)
        last = pl.ds(pl.multiple_of(256 * n + width, 256), 256)
        first = jnp.dot(d_ref[...], normed_ref[:, left], preferred_element_type=jnp.float32)
        second = jnp.dot(d_ref[...], normed_ref[:, right], preferred_element_type=jnp.float32)
        extra = jnp.where(lower, first[main:], second[main:])
        for cols, rows in ((left, first[:main]), (right, second[:main]), (last, extra)):
            packed = rows.astype(jnp.bfloat16).reshape(main // ROW, ROW, 256)
            for copy in range(2):
                o_ref[pl.ds(copy * (main // ROW), main // ROW), :, cols] = packed


def project_and_slot(attended, out_weight, tokens, mod_rows, dispatch):
    rows, width = tokens.shape
    return pl.pallas_call(
        project_kernel,
        out_shape=(
            jax.ShapeDtypeStruct((rows, width), jnp.float32),
            jax.ShapeDtypeStruct((2 * dispatch.shape[0] // 16, ROW, 3 * width // 2), jnp.bfloat16),
        ),
        in_specs=[VM, pl.BlockSpec(memory_space=pl.ANY), VM, VM, VM],
        out_specs=(VM, VM),
        scratch_shapes=[
            pltpu.VMEM((rows, width), jnp.bfloat16),
            pltpu.VMEM((rows, width), jnp.bfloat16),
            pltpu.VMEM((width // 256, width, 256), jnp.bfloat16),
            pltpu.SemaphoreType.DMA((width // 256,)),
        ],
        compiler_params=pltpu.CompilerParams(vmem_limit_bytes=53 << 20),
        cost_estimate=pl.CostEstimate(
            flops=1 << 30, bytes_accessed=12 << 20, transcendentals=1 << 10
        ),
        name="project_and_slot",
    )(attended, out_weight, tokens, mod_rows, dispatch)


def fetch(sources, target, sems):
    return [
        pltpu.make_async_copy(source, target.at[j], sems.at[j])
        for j, source in enumerate(sources)
    ]


def activate(v):
    inner = 0.7978845608028654 * (v + 0.044715 * (v * v * v))
    return (0.5 * v * (1.0 + jnp.tanh(inner))).astype(jnp.bfloat16)


def expert_kernel(x_ref, *refs):
    count = 8
    firsts, seconds = refs[:count], refs[count : 2 * count]
    o_ref, first_buf, second_buf, rows_ref, hidden_ref, out_ref, sems = refs[2 * count :]
    blocks, _, packed = x_ref.shape
    main, width = blocks * ROW, 2048
    half = width // 2
    first_copies = fetch(firsts, first_buf, sems.at[0])
    second_copies = fetch(seconds, second_buf, sems.at[1])
    for copy in first_copies + second_copies:
        copy.start()
    rows_ref[0:main, :] = x_ref[:, :, 0:width].reshape(main, width)
    extra = x_ref[:, :, width:packed].reshape(main, half)
    for h in range(2):
        rows_ref[main:, h * half : (h + 1) * half] = jnp.dot(
            half_rows(h, main), extra, preferred_element_type=jnp.float32
        ).astype(jnp.bfloat16)

    @pl.loop(0, count // 4)
    def _(i):
        for j in (4 * i, 4 * i + 1, 4 * i + 2, 4 * i + 3):
            pltpu.make_async_copy(first_buf.at[j], first_buf.at[j], sems.at[0, j]).wait()
        for j in (4 * i, 4 * i + 1, 4 * i + 2, 4 * i + 3):
            v = jnp.dot(rows_ref[...], first_buf[j], preferred_element_type=jnp.float32)
            hidden_ref[:, pl.ds(pl.multiple_of(256 * j, 256), 256)] = activate(v)

    for copy in second_copies:
        copy.wait()

    @pl.loop(0, width // 1024)
    def _(i):
        for n in (4 * i, 4 * i + 1, 4 * i + 2, 4 * i + 3):
            cols = pl.ds(pl.multiple_of(256 * n, 256), 256)
            out_ref[:, cols] = jnp.dot(
                hidden_ref[...],
                second_buf[:, :, cols].reshape(256 * count, 256),
                preferred_element_type=jnp.float32,
            ).astype(jnp.bfloat16)

    o_ref[:, :, 0:width] = out_ref[0:main, :].reshape(blocks, ROW, width)
    back = None
    for h in range(2):
        part = lax.dot_general(
            half_rows(h, main),
            out_ref[main:, h * half : (h + 1) * half],
            (((0,), (0,)), ((), ())),
            preferred_element_type=jnp.float32,
        )
        back = part if back is None else back + part
    o_ref[:, :, width:packed] = back.astype(jnp.bfloat16).reshape(blocks, ROW, half)


def run_expert(arrived, firsts, seconds):
    rows, count = arrived.shape[0] * (ROW + EXTRA), len(firsts)
    anywhere = pl.BlockSpec(memory_space=pl.ANY)
    return pl.pallas_call(
        expert_kernel,
        out_shape=jax.ShapeDtypeStruct(arrived.shape, jnp.bfloat16),
        in_specs=[VM] + [anywhere] * (2 * count),
        out_specs=VM,
        scratch_shapes=[
            pltpu.VMEM((count, 2048, 256), jnp.bfloat16),
            pltpu.VMEM((count, 256, 2048), jnp.bfloat16),
            pltpu.VMEM((rows, 2048), jnp.bfloat16),
            pltpu.VMEM((rows, 256 * count), jnp.bfloat16),
            pltpu.VMEM((rows, 2048), jnp.bfloat16),
            pltpu.SemaphoreType.DMA((2, count)),
        ],
        compiler_params=pltpu.CompilerParams(vmem_limit_bytes=48 << 20),
        cost_estimate=pl.CostEstimate(
            flops=6 << 30, bytes_accessed=20 << 20, transcendentals=1 << 20
        ),
        name="run_expert",
    )(arrived, *firsts, *seconds)


def finish_kernel(r_ref, g_ref, mixed_ref, gate_ref, o_ref):
    width = mixed_ref.shape[1]
    half = width // 2
    gains = g_ref[...]
    coarse = gains.astype(jnp.bfloat16)
    fine = (gains - coarse.astype(jnp.float32)).astype(jnp.bfloat16)
    both = jnp.concatenate([coarse, fine], axis=0)
    tokens = mixed_ref.shape[0]
    tall = r_ref.shape[0] * ROW
    lane = lax.broadcasted_iota(jnp.int32, (2 * tokens, tall), 1)
    zero = jnp.zeros((2 * tokens, tall), jnp.bfloat16)
    extra = r_ref[:, :, width : width + half].reshape(tall, half)
    for h in range(2):
        main = r_ref[:, :, h * half : (h + 1) * half].reshape(tall, half)
        chosen = jnp.where(((lane >> 2) & 1) == h, both[:, tall:], zero)
        total = jnp.dot(both[:, :tall], main, preferred_element_type=jnp.float32)
        total = total + jnp.dot(chosen, extra, preferred_element_type=jnp.float32)
        cols = slice(h * half, (h + 1) * half)
        combined = total[:tokens] + total[tokens:]
        o_ref[:, cols] = (mixed_ref[:, cols] + gate_ref[:, cols] * combined).astype(jnp.bfloat16)


def finish(returned, gains, mixed, gate):
    return pl.pallas_call(
        finish_kernel,
        out_shape=jax.ShapeDtypeStruct(mixed.shape, jnp.bfloat16),
        in_specs=[VM] * 4,
        out_specs=VM,
        compiler_params=pltpu.CompilerParams(vmem_limit_bytes=20 << 20),
        name="finish",
    )(returned, gains, mixed, gate)


def hop(array, turn):
    layers, cores = lax.axis_size(Z), lax.axis_size("c")
    pairs = []
    for z in range(layers):
        for c in range(cores):
            to = (z + (turn if c else -turn)) % layers
            pairs.append((z * cores + c, to * cores + c))
    return lax.ppermute(array, SEQ, pairs)


def gather_weights(first, second):
    pair = {"first": first, "second": second}
    ahead, behind, far = {}, {}, {}
    for name, w in pair.items():
        ahead[name] = hop(w, 1)
        behind[name] = hop(w, -1)
    for name, w in ahead.items():
        far[name] = hop(w, 1)
    gathered = []
    for name, w in pair.items():
        mine = [w, ahead[name], behind[name], far[name]]
        gathered.append(mine + [step_along(piece, "c", 1) for piece in mine])
    return gathered


def block(
    tokens,
    head_inputs,
    window_ids,
    modulation,
    out_weight,
    expert_in,
    expert_out,
    expert_ids,
    gate_probs,
):
    expert_count = lax.axis_size("exp")
    by_heads = lax.all_to_all(pack(head_inputs[0], window_ids), SEQ, 0, 0, tiled=True)
    firsts, seconds = gather_weights(expert_in[0], expert_out[0])
    attended = attend(by_heads)
    by_tokens = lax.all_to_all(attended, SEQ, 0, 0, tiled=True)
    mod_rows = modulation[0]
    pairs = expert_ids[0]
    pair_experts = pairs.reshape(-1)
    onehot = (pair_experts[:, None] == jnp.arange(expert_count, dtype=jnp.int32)[None, :]).astype(
        jnp.int32
    )
    before = jnp.cumsum(onehot, axis=0) - onehot
    slots = jnp.sum(before * onehot, axis=1).reshape(pairs.shape)
    place = jnp.arange(2 * expert_count * ROW, dtype=jnp.int32)
    owner = (place >> 3) & (expert_count - 1)
    slot = jnp.where(place < expert_count * ROW, place & 7, ROW + (place & 3))
    chosen = (pairs[None] == owner[:, None, None]) & (slots[None] == slot[:, None, None])
    dispatch = jnp.sum(chosen.astype(jnp.int32), axis=2).astype(jnp.bfloat16)
    place = jnp.arange(4 * expert_count * ROW, dtype=jnp.int32)
    owner = (place >> 3) & (expert_count - 1)
    slot = jnp.where(place < 2 * expert_count * ROW, place & 7, ROW + (place & 3))
    picked = (pairs[:, :, None] == owner[None, None]) & (slots[:, :, None] == slot[None, None])
    gains = jnp.sum(jnp.where(picked, gate_probs[0][:, :, None], 0.0), axis=1)
    mixed_rows, outgoing = project_and_slot(by_tokens, out_weight, tokens[0], mod_rows, dispatch)
    arrived = lax.all_to_all(outgoing, FAR, 0, 0, tiled=True)
    outbound = run_expert(arrived, firsts, seconds)
    returned = lax.all_to_all(outbound, FAR, 0, 0, tiled=True)
    return finish(returned, gains, mixed_rows, mod_rows[3][None, :])[None]


def solution(mesh):
    split = Mesh(
        mesh.devices.reshape(2, 4, 2, mesh.shape["exp"]), ("zh", "zl", "c", "exp")
    )
    in_specs = (
        P("exp", SEQ, None),
        P("exp", SEQ, None),
        P("exp", SEQ),
        P("exp", None, None),
        P(),
        P("exp", None, SEQ),
        P("exp", SEQ, None),
        P("exp", SEQ, None),
        P("exp", SEQ, None),
    )
    out_specs = P("exp", SEQ, None)
    return jax.shard_map(block, mesh=split, in_specs=in_specs, out_specs=out_specs, check_vma=False)
```
